32 devices in a mesh: replica: 8 (over y, x, core), fsdp: 4 (over z).
Axes of the slice: x: 2, y: 2, z: 4, core: 2. Of those that a mesh axis runs over, the one named last changes fastest.
Arguments:
- tokens: bfloat16 [6144, 4096], P(('replica', 'fsdp')), may hold values from -6 to 6
- grads_out: bfloat16 [6144, 1024], P(('replica', 'fsdp')), may hold values from -6 to 6
- weights: bfloat16 [8, 4096, 1024], P('replica', 'fsdp'), may hold values from -0.29882812 to 0.29882812
- moments: float32 [8, 4096, 1024], P('replica', 'fsdp'), may hold values from -6 to 6
- step: int32 [1], replicated, may hold values from 0 to 999
Outputs:
- mixed_weights: bfloat16 [8, 4096, 1024], P('replica', 'fsdp')
- new_moments: float32 [8, 4096, 1024], P('replica', 'fsdp')
The draws below stay inside these ranges and needn't reach their ends.
All inputs are finite; a program needn't handle non-finite values.
Results may differ from the reference program's by a relative error of at most 0.001.
Values may be sent and summed in bfloat16 or wider, within the bound.
No kernel may reach another device: no remote copies, remote signals or barrier semaphores. Data moves between devices by JAX's collectives and lax.ppermute only.
A program may use at most 64 MiB of HBM per device.

```python
import jax
import jax.numpy as jnp
from jax import lax

D = 4096
C = 1024
TOKENS = 768
ROWS = 6144
N_REPLICA = 8


def block_scale(key, extent, split, low, largest):
    factor_of = 1.0
    for dim, parts in split:
        draws = jax.random.uniform(jax.random.fold_in(jax.random.fold_in(key, 6), dim), (parts,), jnp.float32, low / len(split), largest / len(split))
        factor_of = factor_of * jnp.repeat(jnp.exp(draws), extent[dim] // parts).reshape((-1,) + (1,) * (len(extent) - 1 - dim))
    return factor_of


def gaussian(rng, extent, spread, reach, shards=(), held_as=jnp.bfloat16):
    entries = spread * jax.random.normal(rng, extent, jnp.float32)
    if shards:
        entries = entries * block_scale(rng, extent, shards, -0.22, 0.18)
    return jnp.clip(entries, -reach, reach).astype(held_as)


def setup_inputs(seed: int = 0) -> dict:
    streams_of = jax.random.split(jax.random.key(seed), 6)
    tokens = gaussian(streams_of[0], (ROWS, D), 1.0, 6.0, ((0, 32),))
    grads_out = gaussian(streams_of[1], (ROWS, C), 1.0, 6.0, ((0, 32),))
    weights = gaussian(streams_of[2], (N_REPLICA, D, C), 0.05, 0.29882812, ((0, 8), (1, 4)))
    moments = gaussian(streams_of[3], (N_REPLICA, D, C), 1.0, 6.0, ((0, 8), (1, 4)), jnp.float32)
    step = jax.random.randint(streams_of[4], (1,), 0, 1000).astype(jnp.int32)
    return dict(tokens=tokens, grads_out=grads_out, weights=weights, moments=moments, step=step)


def one_replica(pair):
    inputs, cotangent = pair
    return jnp.dot(inputs.T, cotangent, preferred_element_type=jnp.float32)


def reference(tokens, grads_out, weights, moments, step):
    inputs = tokens.reshape(N_REPLICA, TOKENS, D)
    cotangent = grads_out.reshape(N_REPLICA, TOKENS, C)
    gradient = lax.map(one_replica, (inputs, cotangent)) * jnp.float32(TOKENS ** -0.5)
    new_moments = 0.9 * moments + gradient
    updated = weights.astype(jnp.float32) - 0.05 * new_moments
    levels = N_REPLICA.bit_length() - 1
    level = (step[0] % levels).astype(jnp.int32)
    distance = jnp.left_shift(jnp.int32(1), level)
    partner = jnp.roll(updated, distance, axis=0)
    mixed_weights = ((updated + partner) * 0.5).astype(jnp.bfloat16)
    return mixed_weights, new_moments
```

```python
from functools import partial

import math
import jax
import jax.numpy as jnp
from jax import lax
from jax.sharding import PartitionSpec as P

SIZES = (1, 1, 1, 1)
FAR = "direct"


def ring(axis, reach):
    count = lax.axis_size(axis)
    return [(i, (i + reach) % count) for i in range(count)]


def after(value, *others):
    return lax.optimization_barrier((value, *others))[0]


def gather_line(block, axis):
    count = lax.axis_size(axis)
    me = lax.axis_index(axis)
    up, down = [block], [block]
    last = count - 1 if FAR == "direct" else count
    for k in range(1, last):
        up.append(lax.ppermute(up[-1], axis, [(i - 1, i) for i in range(k, count)]))
        down.append(lax.ppermute(down[-1], axis, [(i + 1, i) for i in range(count - k)]))
    if FAR == "direct":
        far = lax.ppermute(block, axis, [(0, count - 1), (count - 1, 0)])
        up.append(far)
        down.append(far)
    out = [block]
    for k in range(1, count):
        out.append(jnp.where(me >= k, up[k], down[count - k]))
    return out, [up[1], down[1]]


def gossip(reach, tokens, grads_out, weights, moments):
    shards = lax.axis_size("fsdp")
    me = lax.axis_index("fsdp")
    total_tokens = tokens.shape[0] * shards
    scale = jnp.float32(total_tokens ** (-0.5))
    width = tokens.shape[1] // shards
    limit = 1.0 + 36.0 * 0.05 * total_tokens ** 0.5
    wire = jnp.float32(2.0 ** math.floor(math.log2(60000.0 / limit)))
    unit = width // sum(SIZES)
    grads, hops = gather_line(grads_out, "fsdp")
    grads = jnp.concatenate(grads, 0)
    mixed, news, got = [], [], []
    at = 0
    for c, size in enumerate(SIZES):
        part = size * unit
        source = tokens
        if c == 1:
            source = after(tokens, *hops)
        if c > 1:
            source = after(tokens, *got[c - 2])
        pieces = [
            lax.dynamic_slice_in_dim(source, lax.rem(me + k, shards) * width + at, part, 1)
            for k in range(shards)
        ]
        feats = [pieces[0]]
        for k in range(1, shards):
            feats.append(lax.ppermute(pieces[k], "fsdp", ring("fsdp", k)))
        got.append(feats[1:])
        if c > 0:
            *feats, sent = lax.optimization_barrier((*feats, sent))
        feats = jnp.concatenate(feats, 0)
        rows = slice(at, at + part)
        gradient = lax.dot_general(feats, grads, (((0,), (0,)), ((), ())), preferred_element_type=jnp.float32)
        new = 0.9 * moments[0, rows] + gradient * scale
        updated = weights[0, rows].astype(jnp.float32) - 0.05 * new
        sent = (updated * wire).astype(jnp.float16)
        partner = lax.ppermute(sent, "replica", ring("replica", reach))
        mixed.append((updated, partner))
        news.append(new)
        at += part
    mixed = [((u + p.astype(jnp.float32) * (1.0 / wire)) * 0.5).astype(jnp.bfloat16) for u, p in mixed]
    return jnp.concatenate(mixed, 0)[None], jnp.concatenate(news, 0)[None]


def body(tokens, grads_out, weights, moments, step):
    levels = lax.axis_size("replica").bit_length() - 1
    level = step[0] % levels
    branches = [partial(gossip, 1 << power) for power in range(levels)]
    return lax.switch(level, branches, tokens, grads_out, weights, moments)


def solution(mesh):
    return jax.shard_map(
        body,
        mesh=mesh,
        in_specs=(
            P(("replica", "fsdp"), None),
            P(("replica", "fsdp"), None),
            P("replica", "fsdp", None),
            P("replica", "fsdp", None),
            P(),
        ),
        out_specs=(P("replica", "fsdp", None), P("replica", "fsdp", None)),
        check_vma=False,
    )
```

```python
from functools import partial

import math
import jax
import jax.numpy as jnp
from jax import lax
from jax.sharding import PartitionSpec as P

CUT = 4
SIZES = (1, 1, 1, 1)


def ring(axis, reach):
    count = lax.axis_size(axis)
    return [(i, (i + reach) % count) for i in range(count)]


def across(axis, flip):
    return [(i, i ^ flip) for i in range(lax.axis_size(axis))]


def after(value, *others):
    return lax.optimization_barrier((value, *others))[0]


def gather(block, axis):
    count = lax.axis_size(axis)
    blocks = {0: block}
    for flip in sorted(range(1, count), key=lambda f: (f.bit_count(), -f)):
        low = flip & -flip
        blocks[flip] = lax.ppermute(blocks[flip - low], axis, across(axis, low))
    return [blocks[flip] for flip in range(count)]


def gossip(reach, tokens, grads_out, weights, moments):
    shards = lax.axis_size("fsdp")
    me = lax.axis_index("fsdp")
    total_tokens = tokens.shape[0] * shards
    scale = jnp.float32(total_tokens ** (-0.5))
    width = tokens.shape[1] // shards
    limit = 1.0 + 36.0 * 0.05 * total_tokens ** 0.5
    wire = jnp.float32(2.0 ** math.floor(math.log2(60000.0 / limit)))
    unit = width // sum(SIZES)
    columns = grads_out.shape[1]
    half = columns * CUT // 8
    far = shards // 2

    left = lax.slice_in_dim(grads_out, 0, half, axis=1)
    left = gather(left, "fsdp")
    right = lax.slice_in_dim(after(grads_out, left[far]), half, columns, axis=1)
    right = gather(right, "fsdp")

    def block(feats, grads, rows, cols):
        gradient = lax.dot_general(feats, grads, (((0,), (0,)), ((), ())), preferred_element_type=jnp.float32)
        new = 0.9 * moments[0, rows, cols] + gradient * scale
        updated = weights[0, rows, cols].astype(jnp.float32) - 0.05 * new
        sent = (updated * wire).astype(jnp.float16)
        return new, updated, sent

    def send(sent):
        return lax.ppermute(sent, "replica", ring("replica", reach))

    done, got = [], []
    at = 0
    for c, size in enumerate(SIZES):
        part = size * unit
        source = tokens
        if c == 1:
            source = after(tokens, left[far])
        if c == 2:
            source = after(tokens, left[-1], *got[0])
        if c > 2:
            source = after(tokens, *got[c - 3])
        pieces = [lax.dynamic_slice_in_dim(source, (me ^ k) * width + at, part, 1) for k in range(shards)]
        feats = [pieces[0]]
        for k in range(1, shards):
            feats.append(lax.ppermute(pieces[k], "fsdp", across("fsdp", k)))
        got.append(feats[1:])
        if c > 0:
            *feats, sent = lax.optimization_barrier((*feats, sent))
        feats = jnp.concatenate(feats, 0)
        rows = slice(at, at + part)
        if c == 0:
            new, updated, sent = block(feats, jnp.concatenate(left, 0), rows, slice(0, half))
            done.append((at, 0, new, updated, send(sent)))
            right[-1], feats, sent = lax.optimization_barrier((right[-1], feats, sent))
            new, updated, sent = block(feats, jnp.concatenate(right, 0), rows, slice(half, columns))
            done.append((at, half, new, updated, send(sent)))
            grads = jnp.concatenate([jnp.concatenate([a, b], 1) for a, b in zip(left, right)], 0)
        else:
            new, updated, sent = block(feats, grads, rows, slice(None))
            done.append((at, 0, new, updated, send(sent)))
        at += part
    out = jnp.zeros(weights.shape[1:], weights.dtype)
    new_moments = jnp.zeros(moments.shape[1:], moments.dtype)
    for row, col, new, updated, partner in done:
        mixed = ((updated + partner.astype(jnp.float32) * (1.0 / wire)) * 0.5).astype(jnp.bfloat16)
        out = lax.dynamic_update_slice(out, mixed, (row, col))
        new_moments = lax.dynamic_update_slice(new_moments, new, (row, col))
    return out[None], new_moments[None]


def body(tokens, grads_out, weights, moments, step):
    levels = lax.axis_size("replica").bit_length() - 1
    level = step[0] % levels
    branches = [partial(gossip, 1 << power) for power in range(levels)]
    return lax.switch(level, branches, tokens, grads_out, weights, moments)


def solution(mesh):
    return jax.shard_map(
        body,
        mesh=mesh,
        in_specs=(
            P(("replica", "fsdp"), None),
            P(("replica", "fsdp"), None),
            P("replica", "fsdp", None),
            P("replica", "fsdp", None),
            P(),
        ),
        out_specs=(P("replica", "fsdp", None), P("replica", "fsdp", None)),
        check_vma=False,
    )
```
